256 devices in a mesh: layer: 32 (over y, z_lo, core), dp: 8 (over z_hi, x).
Axes of the slice: x: 4, y: 4, z: 8 (z_hi: 2, z_lo: 4; z = z_hi * 4 + z_lo), core: 2. Of those that a mesh axis runs over, the one named last changes fastest.
Arguments:
- acts: bfloat16 [8192, 32768], P('dp', 'layer'), may hold values from -6 to 6
- grads: bfloat16 [8192, 32768], P('dp', 'layer'), may hold values from -6 to 6
Outputs:
- act_diag: float32 [1024, 32768], P('dp', 'layer')
- grad_diag: float32 [1024, 32768], P('dp', 'layer')
- act_cross: float32 [1024, 32768], P('dp', 'layer')
- grad_cross: float32 [1024, 32768], P('dp', 'layer')
The draws below stay inside these ranges and needn't reach their ends.
All inputs are finite; a program needn't handle non-finite values.
Results may differ from the reference program's by a relative error of at most 0.0003.
Values may be sent and summed in bfloat16 or wider, within the bound.
No kernel may reach another device: no remote copies, remote signals or barrier semaphores. Data moves between devices by JAX's collectives and lax.ppermute only.
A program may use at most 128 MiB of HBM per device.

```python
import jax
import jax.numpy as jnp
from jax import lax

D = 8192
BLK = 1024
LAYERS = 4
TOKENS = 8192


def with_spikes(drawn, rng, source, target, parts, factor):
    owner, partner = [(jnp.arange(drawn.shape[dim]) // (drawn.shape[dim] // parts)).reshape([-1 if axis == dim else 1 for axis in range(drawn.ndim)]) for dim in (source, target)]
    chosen = jax.random.permutation(rng, parts)[partner]
    strong = (owner == chosen) | (owner == (partner + parts // 2) % parts)
    return jnp.where(strong, factor * drawn, drawn)


def shard_levels(rng, dims, cuts, smallest, largest):
    gain = 1.0
    for axis_at, shards_of in cuts:
        draws = jax.random.uniform(jax.random.fold_in(jax.random.fold_in(rng, 6), axis_at), (shards_of,), jnp.float32, smallest / len(cuts), largest / len(cuts))
        gain = gain * jnp.repeat(jnp.exp(draws), dims[axis_at] // shards_of).reshape((-1,) + (1,) * (len(dims) - 1 - axis_at))
    return gain


def bell_draw_with(rng, shape, scale, most, cuts, heavy, kind=jnp.bfloat16):
    entries = scale * jax.random.normal(rng, shape, jnp.float32)
    if cuts:
        entries = entries * shard_levels(rng, shape, cuts, -0.22, 0.18)
    return jnp.clip(with_spikes(entries, jax.random.fold_in(rng, 3), *heavy), -most, most).astype(kind)


def setup_inputs(seed: int = 0) -> dict:
    key_list = jax.random.split(jax.random.key(seed), 3)
    acts = bell_draw_with(key_list[0], (TOKENS, LAYERS * D), 1.0, 6.0, ((0, 8), (1, 32)), (0, 1, 32, 2.75))
    grads = bell_draw_with(key_list[1], (TOKENS, LAYERS * D), 1.0, 6.0, ((0, 8), (1, 32)), (0, 1, 32, 2.75))
    return dict(acts=acts, grads=grads)


def block_stats(left, right):
    left_f = left.astype(jnp.float32)
    right_f = right.astype(jnp.float32)
    return jnp.einsum("tbr,tbc->rbc", left_f, right_f)


def reference(acts, grads):
    tokens_total = acts.shape[0]
    nblk = D // BLK
    act_view = acts.reshape(tokens_total, LAYERS, nblk, BLK)
    grad_view = grads.reshape(tokens_total, LAYERS, nblk, BLK)
    zero_layer = jnp.zeros((tokens_total, 1, nblk, BLK), acts.dtype)
    act_next = jnp.concatenate([act_view[:, 1:], zero_layer], axis=1)
    grad_next = jnp.concatenate([grad_view[:, 1:], zero_layer], axis=1)
    scale = jnp.float32(1.0 / tokens_total)

    def one_layer(index):
        a_here = act_view[:, index]
        g_here = grad_view[:, index]
        a_next = act_next[:, index]
        g_next = grad_next[:, index]
        return (block_stats(a_here, a_here) * scale,
                block_stats(g_here, g_here) * scale,
                block_stats(a_here, a_next) * scale,
                block_stats(g_here, g_next) * scale)

    stacked = lax.map(one_layer, jnp.arange(LAYERS, dtype=jnp.int32))

    def layout(blocks):
        moved = jnp.transpose(blocks, (1, 0, 2, 3))
        return moved.reshape(BLK, LAYERS * D)

    return (layout(stacked[0]), layout(stacked[1]), layout(stacked[2]), layout(stacked[3]))
```

```python
import functools

import jax
import jax.numpy as jnp
from jax import lax
from jax.experimental import pallas as pl
from jax.experimental.pallas import tpu as pltpu
from jax.sharding import PartitionSpec as P

D = 8192
BLK = 128
LANES = 128
HEAD = 16
RING = 4
POWER = 25
SPAN = 1024.0
BASE = 2.0**-5


VMEM = pl.BlockSpec(memory_space=pltpu.VMEM)
SMEM = pl.BlockSpec(memory_space=pltpu.SMEM)
STEP = 32


def unit_of(bound):
    unit = bound * jnp.float32(1.01 / SPAN) + jnp.float32(1e-30)
    return unit.astype(jnp.bfloat16)


def encode(value, gain):
    scaled = value * gain
    lifted = scaled + jnp.where(scaled < 0, jnp.float32(-BASE), jnp.float32(BASE))
    two = lifted * lifted
    four = two * two
    eight = four * four
    return (eight * eight * eight * lifted).astype(jnp.bfloat16)


def decode(code, unit):
    wide = code.astype(jnp.float32)
    size = jnp.maximum(jnp.abs(wide), jnp.float32(BASE**POWER))
    root = jnp.exp2(jnp.log2(size) * jnp.float32(1.0 / POWER) + jnp.float32(5.0))
    grown = root - 1.0
    return jnp.where(wide < 0, -grown, grown) * unit


def lanes_of(unit, rows):
    return jnp.broadcast_to(unit[0:1, :], (rows, LANES))


def head_of(message):
    return message[0:HEAD, :].astype(jnp.float32)[0:8, :]


def block_at(message, piece, groups, group, row):
    start = HEAD + (piece * groups + group) * BLK
    return message[pl.ds(start + row, STEP), :]


def write_head(message, unit):
    message[0:HEAD, :] = jnp.broadcast_to(unit[0:1, :], (HEAD, LANES))


def largest(ref, start, rows, groups):
    def body(i, most):
        for r in range(STEP // 8):
            for g in range(groups):
                part = ref[pl.ds(start + i * STEP + r * 8, 8), pl.ds(g * LANES, LANES)]
                most = jnp.maximum(most, jnp.abs(part))
        return most

    most = lax.fori_loop(0, rows // STEP, body, jnp.zeros((8, LANES), jnp.float32))
    return jnp.broadcast_to(jnp.max(most, keepdims=True), (8, LANES))


def gain_of(unit):
    return jnp.float32(BASE) / unit.astype(jnp.float32)


def fill(message, piece, groups, gain, source):
    wide = lanes_of(gain, STEP)

    def body(i, carry):
        row = pl.multiple_of(i * STEP, STEP)
        for g in range(groups):
            start = HEAD + (piece * groups + g) * BLK
            message[pl.ds(start + row, STEP), :] = encode(source(row, g), wide)
        return carry

    lax.fori_loop(0, BLK // STEP, body, 0)


def rows_of(owner):
    return pl.multiple_of(owner * BLK, BLK)


def around(x, by):
    return lax.rem(x + by + RING, RING)


def tile(ref, start, row, g):
    return ref[pl.ds(start + row, STEP), pl.ds(g * LANES, LANES)]


def first_kernel(at, total, plus, minus, most):
    groups = total.shape[1] // LANES
    x = at[0]
    bound = largest(total, 0, total.shape[0], groups)
    most[...] = bound
    unit = unit_of(bound)
    gain = gain_of(unit)
    write_head(plus, unit)
    write_head(minus, unit)
    far, right, left = around(x, 2), around(x, 1), around(x, -1)
    for message, piece, owner in (
        (plus, 0, far),
        (minus, 0, RING + far),
        (plus, 1, RING + right),
        (minus, 1, left),
    ):
        start = rows_of(owner)
        fill(message, piece, groups, gain, lambda row, g, start=start: tile(total, start, row, g))


def second_kernel(at, total, most, from_left, from_right, plus, minus):
    groups = total.shape[1] // LANES
    x = at[0]
    right, left = around(x, 1), around(x, -1)
    for message, came, owner in ((plus, from_left, right), (minus, from_right, RING + left)):
        start = rows_of(owner)
        head = head_of(came)
        unit = unit_of(most[...] + head * SPAN)
        write_head(message, unit)
        wide = lanes_of(head, STEP)
        fill(
            message,
            0,
            groups,
            gain_of(unit),
            lambda row, g, start=start, came=came, wide=wide: tile(total, start, row, g)
            + decode(block_at(came, 0, groups, g, row), wide),
        )


def gather_ring(at, total, left1, right1, left2, right2, both):
    groups = total.shape[1] // LANES
    x = at[0]
    for half, one, two in ((0, right1, left2), (1, left1, right2)):
        start = rows_of(half * RING + x)
        wide1, wide2 = lanes_of(head_of(one), STEP), lanes_of(head_of(two), STEP)

        def body(i, carry, half=half, one=one, two=two, start=start, wide1=wide1, wide2=wide2):
            row = pl.multiple_of(i * STEP, STEP)
            for g in range(groups):
                both[pl.ds(half * BLK + row, STEP), pl.ds(g * LANES, LANES)] = (
                    tile(total, start, row, g)
                    + decode(block_at(one, 1, groups, g, row), wide1)
                    + decode(block_at(two, 0, groups, g, row), wide2)
                )
            return carry

        lax.fori_loop(0, BLK // STEP, body, 0)


def send_rows(both, start, message):
    groups = both.shape[1] // LANES
    unit = unit_of(largest(both, start, BLK, groups))
    write_head(message, unit)
    fill(message, 0, groups, gain_of(unit), lambda row, g: tile(both, start, row, g))


def third_kernel(at, total, left1, right1, left2, right2, kept, message, both):
    gather_ring(at, total, left1, right1, left2, right2, both)
    half = at[1]
    kept[...] = both[pl.ds(rows_of(half), BLK), :]
    send_rows(both, rows_of(1 - half), message)


def third_kernel_away(at, total, left1, right1, left2, right2, same, message, both):
    gather_ring(at, total, left1, right1, left2, right2, both)
    half = at[1]
    send_rows(both, rows_of(1 - half), message)
    send_rows(both, rows_of(half), same)


def last_kernel(scale, *refs):
    out = refs[-1]
    column = 0
    for kept, message in zip(refs[:-1:2], refs[1:-1:2]):
        plain = kept.dtype == jnp.float32
        groups = (message.shape[0] - HEAD) // BLK
        wide = lanes_of(head_of(message), STEP)
        wide_kept = None if plain else lanes_of(head_of(kept), STEP)

        def body(i, carry, kept=kept, message=message, groups=groups, wide=wide,
                 wide_kept=wide_kept, plain=plain, column=column):
            row = pl.multiple_of(i * STEP, STEP)
            for g in range(groups):
                if plain:
                    mine = tile(kept, 0, row, g)
                else:
                    mine = decode(block_at(kept, 0, groups, g, row), wide_kept)
                value = (mine + decode(block_at(message, 0, groups, g, row), wide)) * scale[0]
                out[pl.ds(row, STEP), pl.ds((column + g) * LANES, LANES)] = value
            return carry

        lax.fori_loop(0, BLK // STEP, body, 0)
        column += groups


def call(kernel, ins, outs, scratch=(), name=None):
    return pl.pallas_call(
        kernel,
        out_shape=outs,
        in_specs=[SMEM] + [VMEM] * (len(ins) - 1),
        out_specs=[VMEM] * len(outs),
        scratch_shapes=list(scratch),
        compiler_params=pltpu.CompilerParams(vmem_limit_bytes=LIMIT),
        name=name,
    )(*ins)


LIMIT = 20 * 2**20


def message_shape(pieces, width):
    return jax.ShapeDtypeStruct((HEAD + pieces * width, LANES), jnp.bfloat16)


def inner_tokens(left, right):
    return lax.dot_general(
        left, right, (((0,), (0,)), ((), ())), preferred_element_type=jnp.float32
    )


def on_device(acts, grads):
    width = acts.shape[1]
    per_layer = D // width
    shards = lax.axis_size("dp")
    spots = lax.axis_size("layer")
    f32 = jnp.float32
    place = lax.axis_index("dp")
    at = jnp.stack([lax.rem(place, RING), lax.div(place, RING)]).astype(jnp.int32)
    scale = f32(1.0 / (acts.shape[0] * shards))
    last = lax.axis_index("layer") >= spots - per_layer
    plain_scale = jnp.full((1,), scale, f32)
    cross_scale = jnp.where(last, f32(0), scale).reshape(1)

    ring = [
        [(z * RING + x, z * RING + (x + by) % RING) for z in range(shards // RING) for x in range(RING)]
        for by in (1, -1)
    ]
    flip = [(d, (d + RING) % shards) for d in range(shards)]
    down = [(l, l - per_layer) for l in range(per_layer, spots)]
    up = [(l - per_layer, l) for l in range(per_layer, spots)]
    down_flip = [
        (l * shards + d, (l - per_layer) * shards + (d + RING) % shards)
        for l in range(per_layer, spots)
        for d in range(shards)
    ]

    half = width // 2
    next_a = lax.ppermute(acts[:, :half], "layer", down)
    prev_g = lax.ppermute(grads, "layer", up)
    next_b = lax.ppermute(acts[:, half:], "layer", down)

    def first(total):
        cols = total.shape[1]
        plus, minus, most = call(
            first_kernel, (at, total),
            (message_shape(2, cols), message_shape(2, cols), jax.ShapeDtypeStruct((8, LANES), f32)),
        )
        return total, most, lax.ppermute(plus, "dp", ring[0]), lax.ppermute(minus, "dp", ring[1])

    def second(state):
        total, most, left1, right1 = state
        cols = total.shape[1]
        plus, minus = call(
            second_kernel, (at, total, most, left1, right1),
            (message_shape(1, cols), message_shape(1, cols)),
        )
        return total, left1, right1, lax.ppermute(plus, "dp", ring[0]), lax.ppermute(minus, "dp", ring[1])

    def third(state, away=False):
        total = state[0]
        cols = total.shape[1]
        scratch = (pltpu.VMEM((2 * BLK, cols), f32),)
        if away:
            same, message = call(
                third_kernel_away, (at,) + state, (message_shape(1, cols),) * 2, scratch
            )
            return (
                lax.ppermute(same, "layer", down),
                lax.ppermute(message, ("layer", "dp"), down_flip),
            )
        kept, message = call(
            third_kernel, (at,) + state,
            (jax.ShapeDtypeStruct((BLK, cols), f32), message_shape(1, cols)), scratch,
        )
        return kept, lax.ppermute(message, "dp", flip)

    def finish(factor, *pairs):
        return call(
            last_kernel, (factor,) + pairs, (jax.ShapeDtypeStruct((BLK, width), f32),)
        )[0]

    one = first(inner_tokens(acts, acts))
    two = first(inner_tokens(grads, grads))
    one = second(one)
    three = first(inner_tokens(acts, next_a))
    two = second(two)
    one = third(one)
    four = first(inner_tokens(prev_g, grads))
    three = second(three)
    two = third(two)
    five = first(inner_tokens(acts, next_b))
    four = second(four)
    three = third(three)
    act_diag = finish(plain_scale, *one)
    five = second(five)
    four = third(four, away=True)
    grad_diag = finish(plain_scale, *two)
    five = third(five)
    grad_cross = finish(plain_scale, *four)
    act_cross = finish(cross_scale, *(three + five))
    return (act_diag, grad_diag, act_cross, grad_cross)


def solution(mesh):
    spec = P("dp", "layer")
    return jax.shard_map(
        on_device, mesh=mesh, in_specs=(spec,) * 2, out_specs=(spec,) * 4, check_vma=False
    )
```

```python
import jax
import jax.numpy as jnp
from jax import lax
from jax.experimental import pallas as pl
from jax.experimental.pallas import tpu as pltpu
from jax.sharding import PartitionSpec as P


D = 8192
BLK = 128
LANES = 128
HEAD = 16
RING = 4
POWER = 25
SPAN = 1024.0
BASE = 2.0**-5


VMEM = pl.BlockSpec(memory_space=pltpu.VMEM)
SMEM = pl.BlockSpec(memory_space=pltpu.SMEM)
STEP = 32


def unit_of(bound):
    unit = bound * jnp.float32(1.01 / SPAN) + jnp.float32(1e-30)
    return unit.astype(jnp.bfloat16)


def encode(value, gain):
    scaled = value * gain
    lifted = scaled + jnp.where(scaled < 0, jnp.float32(-BASE), jnp.float32(BASE))
    two = lifted * lifted
    four = two * two
    eight = four * four
    return (eight * eight * eight * lifted).astype(jnp.bfloat16)


def decode(code, unit):
    wide = code.astype(jnp.float32)
    size = jnp.maximum(jnp.abs(wide), jnp.float32(BASE**POWER))
    root = jnp.exp2(jnp.log2(size) * jnp.float32(1.0 / POWER) + jnp.float32(5.0))
    grown = root - 1.0
    return jnp.where(wide < 0, -grown, grown) * unit


def lanes_of(unit, rows):
    return jnp.broadcast_to(unit[0:1, :], (rows, LANES))


def head_of(message):
    return message[0:HEAD, :].astype(jnp.float32)[0:8, :]


def block_at(message, piece, groups, group, row):
    start = HEAD + (piece * groups + group) * BLK
    return message[pl.ds(start + row, STEP), :]


def write_head(message, unit):
    message[0:HEAD, :] = jnp.broadcast_to(unit[0:1, :], (HEAD, LANES))


def largest(ref, start, rows, groups):
    def body(i, most):
        for r in range(STEP // 8):
            for g in range(groups):
                part = ref[pl.ds(start + i * STEP + r * 8, 8), pl.ds(g * LANES, LANES)]
                most = jnp.maximum(most, jnp.abs(part))
        return most

    most = lax.fori_loop(0, rows // STEP, body, jnp.zeros((8, LANES), jnp.float32))
    return jnp.broadcast_to(jnp.max(most, keepdims=True), (8, LANES))


def gain_of(unit):
    return jnp.float32(BASE) / unit.astype(jnp.float32)


def fill(message, piece, groups, gain, source):
    wide = lanes_of(gain, STEP)

    def body(i, carry):
        row = pl.multiple_of(i * STEP, STEP)
        for g in range(groups):
            start = HEAD + (piece * groups + g) * BLK
            message[pl.ds(start + row, STEP), :] = encode(source(row, g), wide)
        return carry

    lax.fori_loop(0, BLK // STEP, body, 0)


def rows_of(owner):
    return pl.multiple_of(owner * BLK, BLK)


def around(x, by):
    return lax.rem(x + by + RING, RING)


def tile(ref, start, row, g):
    return ref[pl.ds(start + row, STEP), pl.ds(g * LANES, LANES)]


def first_kernel(at, total, plus, minus, most):
    groups = total.shape[1] // LANES
    x = at[0]
    bound = largest(total, 0, total.shape[0], groups)
    most[...] = bound
    unit = unit_of(bound)
    gain = gain_of(unit)
    write_head(plus, unit)
    write_head(minus, unit)
    far, right, left = around(x, 2), around(x, 1), around(x, -1)
    for message, piece, owner in (
        (plus, 0, far),
        (minus, 0, RING + far),
        (plus, 1, RING + right),
        (minus, 1, left),
    ):
        start = rows_of(owner)
        fill(message, piece, groups, gain, lambda row, g, start=start: tile(total, start, row, g))


def second_kernel(at, total, most, from_left, from_right, plus, minus):
    groups = total.shape[1] // LANES
    x = at[0]
    right, left = around(x, 1), around(x, -1)
    for message, came, owner in ((plus, from_left, right), (minus, from_right, RING + left)):
        start = rows_of(owner)
        head = head_of(came)
        unit = unit_of(most[...] + head * SPAN)
        write_head(message, unit)
        wide = lanes_of(head, STEP)
        fill(
            message,
            0,
            groups,
            gain_of(unit),
            lambda row, g, start=start, came=came, wide=wide: tile(total, start, row, g)
            + decode(block_at(came, 0, groups, g, row), wide),
        )


def gather_ring(at, total, left1, right1, left2, right2, both):
    groups = total.shape[1] // LANES
    x = at[0]
    for half, one, two in ((0, right1, left2), (1, left1, right2)):
        start = rows_of(half * RING + x)
        wide1, wide2 = lanes_of(head_of(one), STEP), lanes_of(head_of(two), STEP)

        def body(i, carry, half=half, one=one, two=two, start=start, wide1=wide1, wide2=wide2):
            row = pl.multiple_of(i * STEP, STEP)
            for g in range(groups):
                both[pl.ds(half * BLK + row, STEP), pl.ds(g * LANES, LANES)] = (
                    tile(total, start, row, g)
                    + decode(block_at(one, 1, groups, g, row), wide1)
                    + decode(block_at(two, 0, groups, g, row), wide2)
                )
            return carry

        lax.fori_loop(0, BLK // STEP, body, 0)


def send_rows(both, start, message):
    groups = both.shape[1] // LANES
    unit = unit_of(largest(both, start, BLK, groups))
    write_head(message, unit)
    fill(message, 0, groups, gain_of(unit), lambda row, g: tile(both, start, row, g))


def third_kernel(at, total, left1, right1, left2, right2, kept, message, both):
    gather_ring(at, total, left1, right1, left2, right2, both)
    half = at[1]
    send_rows(both, rows_of(1 - half), message)
    kept[...] = both[pl.ds(rows_of(half), BLK), :]


def same_kernel(at, before, kept, same):
    @pl.when(at[2] == 0)
    def _():
        send_rows(kept, 0, same)

    @pl.when(at[2] != 0)
    def _():
        send_rows(before, 0, same)


def add_up(out, kept, message, scale):
    groups = out.shape[1] // LANES
    plain = kept.dtype == jnp.float32
    wide = lanes_of(head_of(message), STEP)
    wide_kept = None if plain else lanes_of(head_of(kept), STEP)

    def body(i, carry):
        row = pl.multiple_of(i * STEP, STEP)
        for g in range(groups):
            if plain:
                mine = tile(kept, 0, row, g)
            else:
                mine = decode(block_at(kept, 0, groups, g, row), wide_kept)
            value = (mine + decode(block_at(message, 0, groups, g, row), wide)) * scale
            out[pl.ds(row, STEP), pl.ds(g * LANES, LANES)] = value
        return carry

    lax.fori_loop(0, BLK // STEP, body, 0)


def last_kernel(scale, kept, message, out):
    add_up(out, kept, message, scale[0])


def last_kernel_cross(scale, at, kept1, other1, kept2, other2, same, act, grad):
    @pl.when(at[0] == 0)
    def _():
        add_up(act, kept1, other1, scale[0])
        add_up(grad, same, other2, scale[0])

    @pl.when(at[0] != 0)
    def _():
        add_up(act, kept2, other2, scale[0])
        add_up(grad, same, other1, scale[0])


def call(kernel, ins, outs, scratch=(), scalars=1):
    return pl.pallas_call(
        kernel,
        out_shape=outs,
        in_specs=[SMEM] * scalars + [VMEM] * (len(ins) - scalars),
        out_specs=[VMEM] * len(outs),
        scratch_shapes=list(scratch),
        compiler_params=pltpu.CompilerParams(vmem_limit_bytes=LIMIT),
    )(*ins)


LIMIT = 20 * 2**20


def message_shape(pieces, width):
    return jax.ShapeDtypeStruct((HEAD + pieces * width, LANES), jnp.bfloat16)


def inner_tokens(left, right):
    return lax.dot_general(
        left, right, (((0,), (0,)), ((), ())), preferred_element_type=jnp.float32
    )


def statistics(acts, grads):
    width = acts.shape[1]
    per_layer = D // width
    shards = lax.axis_size("dp")
    spots = lax.axis_size("layer")
    f32 = jnp.float32
    place = lax.axis_index("dp")
    spot = lax.axis_index("layer")
    core = lax.rem(spot, 2)
    at = jnp.stack([lax.rem(place, RING), lax.div(place, RING), core]).astype(jnp.int32)
    scale = f32(1.0 / (acts.shape[0] * shards))
    plain_scale = jnp.full((1,), scale, f32)
    cross_scale = jnp.where(spot >= spots - per_layer, f32(0), scale).reshape(1)
    even = core == 0

    ring = [
        [(z * RING + x, z * RING + (x + by) % RING) for z in range(shards // RING) for x in range(RING)]
        for by in (1, -1)
    ]
    flip = [(d, (d + RING) % shards) for d in range(shards)]
    down = [(l, l - per_layer) for l in range(per_layer, spots)]

    def moves(parity, by):
        return [
            (l, l + by * per_layer)
            for l in range(spots)
            if l % 2 == parity and 0 <= l + by * per_layer < spots
        ]

    def across(parity):
        for l in range(spots):
            to = l if l % 2 == parity else l - per_layer
            if 0 <= to:
                for d in range(shards):
                    yield (l * shards + d, to * shards + (d + RING) % shards)

    def first(total):
        cols = total.shape[1]
        plus, minus, most = call(
            first_kernel, (at, total),
            (message_shape(2, cols), message_shape(2, cols), jax.ShapeDtypeStruct((8, LANES), f32)),
        )
        return (
            total, most,
            lax.ppermute(plus, "dp", ring[0]),
            lax.ppermute(minus, "dp", ring[1]),
        )

    def second(state):
        total, most, left1, right1 = state
        cols = total.shape[1]
        plus, minus = call(
            second_kernel, (at, total, most, left1, right1),
            (message_shape(1, cols), message_shape(1, cols)),
        )
        return (
            total, left1, right1,
            lax.ppermute(plus, "dp", ring[0]),
            lax.ppermute(minus, "dp", ring[1]),
        )

    def third(state):
        cols = state[0].shape[1]
        outs = (jax.ShapeDtypeStruct((BLK, cols), f32), message_shape(1, cols))
        scratch = (pltpu.VMEM((2 * BLK, cols), f32),)
        return call(third_kernel, (at,) + state, outs, scratch)

    acts_in = lax.ppermute(acts, "layer", moves(0, -1))
    grads_in = lax.ppermute(grads, "layer", moves(1, 1))
    u1 = first(inner_tokens(acts, acts))
    u2 = first(inner_tokens(grads, grads))
    u1 = second(u1)
    grads_in_later = lax.ppermute(grads, "layer", moves(0, 1))
    acts_in_later = lax.ppermute(acts, "layer", moves(1, -1))
    v1 = inner_tokens(jnp.where(even, acts, grads_in), jnp.where(even, acts_in, grads))
    v1 = first(v1)
    u2 = second(u2)
    kept_u1, out_u1 = third(u1)
    in_u1 = lax.ppermute(out_u1, "dp", flip)
    v1 = second(v1)
    v2 = inner_tokens(jnp.where(even, grads_in_later, acts), jnp.where(even, grads, acts_in_later))
    v2 = first(v2)
    kept_u2, out_u2 = third(u2)
    in_u2 = lax.ppermute(out_u2, "dp", flip)
    v2 = second(v2)
    kept_v1, out_v1 = third(v1)
    in_v1 = lax.ppermute(out_v1, ("layer", "dp"), list(across(0)))
    kept_v2, out_v2 = third(v2)
    in_v2 = lax.ppermute(out_v2, ("layer", "dp"), list(across(1)))
    same = call(same_kernel, (at, kept_v1, kept_v2), (message_shape(1, width),))[0]
    same_in = lax.ppermute(same, "layer", down)

    out_shape = jax.ShapeDtypeStruct((BLK, width), f32)
    act_diag = call(last_kernel, (plain_scale, kept_u1, in_u1), (out_shape,))[0]
    grad_diag = call(last_kernel, (plain_scale, kept_u2, in_u2), (out_shape,))[0]
    act_cross, grad_cross = call(
        last_kernel_cross,
        (cross_scale, core.reshape(1).astype(jnp.int32), kept_v1, in_v1, kept_v2, in_v2, same_in),
        (out_shape,) * 2, scalars=2,
    )
    return (act_diag, grad_diag, act_cross, grad_cross)


def solution(mesh):
    spec = P("dp", "layer")
    return jax.shard_map(
        statistics, mesh=mesh, in_specs=(spec,) * 2, out_specs=(spec,) * 4, check_vma=False
    )
```

```python
import jax
import jax.numpy as jnp
from jax import lax
from jax.experimental import pallas as pl
from jax.experimental.pallas import tpu as pltpu
from jax.sharding import PartitionSpec as P


D = 8192
BLK = 128
LANES = 128
HEAD = 16
RING = 4
POWER = 25
SPAN = 1024.0
BASE = 2.0**-5


VMEM = pl.BlockSpec(memory_space=pltpu.VMEM)
SMEM = pl.BlockSpec(memory_space=pltpu.SMEM)
STEP = 32


def unit_of(bound):
    unit = bound * jnp.float32(1.01 / SPAN) + jnp.float32(1e-30)
    return unit.astype(jnp.bfloat16)


def encode(value, gain):
    scaled = value * gain
    lifted = scaled + jnp.where(scaled < 0, jnp.float32(-BASE), jnp.float32(BASE))
    two = lifted * lifted
    four = two * two
    eight = four * four
    return (eight * eight * eight * lifted).astype(jnp.bfloat16)


def decode(code, unit):
    wide = code.astype(jnp.float32)
    size = jnp.maximum(jnp.abs(wide), jnp.float32(BASE**POWER))
    root = jnp.exp2(jnp.log2(size) * jnp.float32(1.0 / POWER) + jnp.float32(5.0))
    grown = root - 1.0
    return jnp.where(wide < 0, -grown, grown) * unit


def lanes_of(unit, rows):
    return jnp.broadcast_to(unit[0:1, :], (rows, LANES))


def head_of(message):
    return message[0:HEAD, :].astype(jnp.float32)[0:8, :]


def block_at(message, piece, groups, group, row):
    start = HEAD + (piece * groups + group) * BLK
    return message[pl.ds(start + row, STEP), :]


def write_head(message, unit):
    message[0:HEAD, :] = jnp.broadcast_to(unit[0:1, :], (HEAD, LANES))


def largest(ref, start, rows, groups):
    def body(i, most):
        for r in range(STEP // 8):
            for g in range(groups):
                part = ref[pl.ds(start + i * STEP + r * 8, 8), pl.ds(g * LANES, LANES)]
                most = jnp.maximum(most, jnp.abs(part))
        return most

    most = lax.fori_loop(0, rows // STEP, body, jnp.zeros((8, LANES), jnp.float32))
    return jnp.broadcast_to(jnp.max(most, keepdims=True), (8, LANES))


def gain_of(unit):
    return jnp.float32(BASE) / unit.astype(jnp.float32)


def fill(message, piece, groups, gain, source):
    wide = lanes_of(gain, STEP)

    def body(i, carry):
        row = pl.multiple_of(i * STEP, STEP)
        for g in range(groups):
            start = HEAD + (piece * groups + g) * BLK
            message[pl.ds(start + row, STEP), :] = encode(source(row, g), wide)
        return carry

    lax.fori_loop(0, BLK // STEP, body, 0)


def rows_of(owner):
    return pl.multiple_of(owner * BLK, BLK)


def around(x, by):
    return lax.rem(x + by + RING, RING)


def tile(ref, start, row, g):
    return ref[pl.ds(start + row, STEP), pl.ds(g * LANES, LANES)]


def first_kernel(at, total, plus, minus, most):
    groups = total.shape[1] // LANES
    x = at[0]
    bound = largest(total, 0, total.shape[0], groups)
    most[...] = bound
    unit = unit_of(bound)
    gain = gain_of(unit)
    write_head(plus, unit)
    write_head(minus, unit)
    far, right, left = around(x, 2), around(x, 1), around(x, -1)
    for message, piece, owner in (
        (plus, 0, far),
        (minus, 0, RING + far),
        (plus, 1, RING + right),
        (minus, 1, left),
    ):
        start = rows_of(owner)
        fill(message, piece, groups, gain, lambda row, g, start=start: tile(total, start, row, g))


def second_kernel(at, total, most, from_left, from_right, plus, minus):
    groups = total.shape[1] // LANES
    x = at[0]
    right, left = around(x, 1), around(x, -1)
    for message, came, owner in ((plus, from_left, right), (minus, from_right, RING + left)):
        start = rows_of(owner)
        head = head_of(came)
        unit = unit_of(most[...] + head * SPAN)
        write_head(message, unit)
        wide = lanes_of(head, STEP)
        fill(
            message,
            0,
            groups,
            gain_of(unit),
            lambda row, g, start=start, came=came, wide=wide: tile(total, start, row, g)
            + decode(block_at(came, 0, groups, g, row), wide),
        )


def gather_ring(at, total, left1, right1, left2, right2, both):
    groups = total.shape[1] // LANES
    x = at[0]
    for half, one, two in ((0, right1, left2), (1, left1, right2)):
        start = rows_of(half * RING + x)
        wide1, wide2 = lanes_of(head_of(one), STEP), lanes_of(head_of(two), STEP)

        def body(i, carry, half=half, one=one, two=two, start=start, wide1=wide1, wide2=wide2):
            row = pl.multiple_of(i * STEP, STEP)
            for g in range(groups):
                both[pl.ds(half * BLK + row, STEP), pl.ds(g * LANES, LANES)] = (
                    tile(total, start, row, g)
                    + decode(block_at(one, 1, groups, g, row), wide1)
                    + decode(block_at(two, 0, groups, g, row), wide2)
                )
            return carry

        lax.fori_loop(0, BLK // STEP, body, 0)


def send_rows(both, start, message):
    groups = both.shape[1] // LANES
    unit = unit_of(largest(both, start, BLK, groups))
    write_head(message, unit)
    fill(message, 0, groups, gain_of(unit), lambda row, g: tile(both, start, row, g))


def third_kernel(at, total, left1, right1, left2, right2, kept, message, both):
    gather_ring(at, total, left1, right1, left2, right2, both)
    half = at[1]
    send_rows(both, rows_of(1 - half), message)
    kept[...] = both[pl.ds(rows_of(half), BLK), :]


def third_kernel_away(
    at, total, left1, right1, left2, right2, before, kept, message, same, both
):
    third_kernel(at, total, left1, right1, left2, right2, kept, message, both)

    @pl.when(at[2] == 0)
    def _():
        send_rows(kept, 0, same)

    @pl.when(at[2] != 0)
    def _():
        send_rows(before, 0, same)


def add_up(out, kept, message, scale):
    groups = out.shape[1] // LANES
    plain = kept.dtype == jnp.float32
    wide = lanes_of(head_of(message), STEP)
    wide_kept = None if plain else lanes_of(head_of(kept), STEP)

    def body(i, carry):
        row = pl.multiple_of(i * STEP, STEP)
        for g in range(groups):
            if plain:
                mine = tile(kept, 0, row, g)
            else:
                mine = decode(block_at(kept, 0, groups, g, row), wide_kept)
            value = (mine + decode(block_at(message, 0, groups, g, row), wide)) * scale
            out[pl.ds(row, STEP), pl.ds(g * LANES, LANES)] = value
        return carry

    lax.fori_loop(0, BLK // STEP, body, 0)


def last_kernel(scale, kept, message, out):
    add_up(out, kept, message, scale[0])


def last_kernel_cross(scale, at, kept1, other1, kept2, other2, same, act, grad):
    @pl.when(at[0] == 0)
    def _():
        add_up(act, kept1, other1, scale[0])
        add_up(grad, same, other2, scale[0])

    @pl.when(at[0] != 0)
    def _():
        add_up(act, kept2, other2, scale[0])
        add_up(grad, same, other1, scale[0])


def call(kernel, ins, outs, scratch=(), scalars=1):
    return pl.pallas_call(
        kernel,
        out_shape=outs,
        in_specs=[SMEM] * scalars + [VMEM] * (len(ins) - scalars),
        out_specs=[VMEM] * len(outs),
        scratch_shapes=list(scratch),
        compiler_params=pltpu.CompilerParams(vmem_limit_bytes=LIMIT),
    )(*ins)


LIMIT = 20 * 2**20


def message_shape(pieces, width):
    return jax.ShapeDtypeStruct((HEAD + pieces * width, LANES), jnp.bfloat16)


def inner_tokens(left, right):
    return lax.dot_general(
        left, right, (((0,), (0,)), ((), ())), preferred_element_type=jnp.float32
    )


def statistics(acts, grads):
    width = acts.shape[1]
    per_layer = D // width
    shards = lax.axis_size("dp")
    spots = lax.axis_size("layer")
    f32 = jnp.float32
    place = lax.axis_index("dp")
    spot = lax.axis_index("layer")
    core = lax.rem(spot, 2)
    at = jnp.stack([lax.rem(place, RING), lax.div(place, RING), core]).astype(jnp.int32)
    scale = f32(1.0 / (acts.shape[0] * shards))
    plain_scale = jnp.full((1,), scale, f32)
    cross_scale = jnp.where(spot >= spots - per_layer, f32(0), scale).reshape(1)
    even = core == 0

    ring = [
        [(z * RING + x, z * RING + (x + by) % RING) for z in range(shards // RING) for x in range(RING)]
        for by in (1, -1)
    ]
    flip = [(d, (d + RING) % shards) for d in range(shards)]
    down = [(l, l - per_layer) for l in range(per_layer, spots)]

    def moves(parity, by):
        return [
            (l, l + by * per_layer)
            for l in range(spots)
            if l % 2 == parity and 0 <= l + by * per_layer < spots
        ]

    def across(parity):
        for l in range(spots):
            to = l if l % 2 == parity else l - per_layer
            if 0 <= to:
                for d in range(shards):
                    yield (l * shards + d, to * shards + (d + RING) % shards)

    def first(total):
        cols = total.shape[1]
        plus, minus, most = call(
            first_kernel, (at, total),
            (message_shape(2, cols), message_shape(2, cols), jax.ShapeDtypeStruct((8, LANES), f32)),
        )
        return (
            total, most,
            lax.ppermute(plus, "dp", ring[0]),
            lax.ppermute(minus, "dp", ring[1]),
        )

    def second(state):
        total, most, left1, right1 = state
        cols = total.shape[1]
        plus, minus = call(
            second_kernel, (at, total, most, left1, right1),
            (message_shape(1, cols), message_shape(1, cols)),
        )
        return (
            total, left1, right1,
            lax.ppermute(plus, "dp", ring[0]),
            lax.ppermute(minus, "dp", ring[1]),
        )

    def third(state, before=None):
        cols = state[0].shape[1]
        outs = (jax.ShapeDtypeStruct((BLK, cols), f32), message_shape(1, cols))
        scratch = (pltpu.VMEM((2 * BLK, cols), f32),)
        if before is None:
            return call(third_kernel, (at,) + state, outs, scratch)
        return call(
            third_kernel_away, (at,) + state + (before,),
            outs + (message_shape(1, cols),), scratch,
        )

    lead = jnp.where(even, acts, grads)
    lead_in = lax.ppermute(lead, "layer", moves(0, -1) + moves(1, 1))
    u1 = first(inner_tokens(acts, acts))
    u2 = first(inner_tokens(grads, grads))
    token = u1[1]
    u1 = second(u1)
    acts_again, grads_again, _ = lax.optimization_barrier((acts, grads, token))
    follow = jnp.where(even, grads_again, acts_again)
    follow_in = lax.ppermute(follow, "layer", moves(0, 1) + moves(1, -1))
    v1 = inner_tokens(jnp.where(even, lead, lead_in), jnp.where(even, lead_in, lead))
    v1 = first(v1)
    u2 = second(u2)
    kept_u1, out_u1 = third(u1)
    in_u1 = lax.ppermute(out_u1, "dp", flip)
    v1 = second(v1)
    v2 = inner_tokens(jnp.where(even, follow_in, follow), jnp.where(even, follow, follow_in))
    v2 = first(v2)
    kept_u2, out_u2 = third(u2)
    in_u2 = lax.ppermute(out_u2, "dp", flip)
    v2 = second(v2)
    kept_v1, out_v1 = third(v1)
    in_v1 = lax.ppermute(out_v1, ("layer", "dp"), list(across(0)))
    kept_v2, out_v2, same = third(v2, kept_v1)
    in_v2 = lax.ppermute(out_v2, ("layer", "dp"), list(across(1)))
    same_in = lax.ppermute(same, "layer", down)

    out_shape = jax.ShapeDtypeStruct((BLK, width), f32)
    act_diag = call(last_kernel, (plain_scale, kept_u1, in_u1), (out_shape,))[0]
    grad_diag = call(last_kernel, (plain_scale, kept_u2, in_u2), (out_shape,))[0]
    act_cross, grad_cross = call(
        last_kernel_cross,
        (cross_scale, core.reshape(1).astype(jnp.int32), kept_v1, in_v1, kept_v2, in_v2, same_in),
        (out_shape,) * 2, scalars=2,
    )
    return (act_diag, grad_diag, act_cross, grad_cross)


def solution(mesh):
    spec = P("dp", "layer")
    return jax.shard_map(
        statistics, mesh=mesh, in_specs=(spec,) * 2, out_specs=(spec,) * 4, check_vma=False
    )
```
